32 devices in a mesh: cohort: 4 (over x, core), fsdp: 8 (over z, y).
Axes of the slice: x: 2, y: 2, z: 4, core: 2. Of those that a mesh axis runs over, the one named last changes fastest.
Arguments:
- client_tokens: bfloat16 [4, 4, 2, 64, 3584], P('cohort', None, None, 'fsdp'), may hold values from -18 to 18
- targets: bfloat16 [4, 4, 2, 64, 7168], P('cohort', None, None, None, 'fsdp'), may hold values from -12 to 12
- weights: bfloat16 [7168, 3584], P('fsdp'), may hold values from -6 to 6
- momentum: float32 [7168, 3584], P('fsdp', 'cohort'), may hold values from -2 to 2
- noise_now: bfloat16 [7168, 3584], P('fsdp', 'cohort'), may hold values from -6 to 6
- noise_prev: bfloat16 [7168, 3584], P('fsdp', 'cohort'), may hold values from -6 to 6
Outputs:
- new_weights: bfloat16 [7168, 3584], P('fsdp')
- new_momentum: float32 [7168, 3584], P('fsdp', 'cohort')
The draws below stay inside these ranges and needn't reach their ends.
All inputs are finite; a program needn't handle non-finite values.
Results may differ from the reference program's by a relative error of at most 0.0028.
The reference program's roundings to bfloat16 on the way (of `error_term` and `current`) count: a program that leaves them out, or rounds other values in their place, can miss the bound.
Values may be sent and summed in bfloat16 or wider, within the bound.
A program may use at most 128 MiB of HBM per device.

```python
import math
import jax
import jax.numpy as jnp
from jax import lax

D = 3584
FF = 7168
CLIENTS = 4
STEPS = 2
STEP_TOKENS = 64
COHORTS = 4


def draw_client_tokens(key, part):
    first, second, third = jax.random.split(key, 3)
    shape = (COHORTS, CLIENTS, STEPS, STEP_TOKENS, D)
    columns = jnp.exp(jax.random.uniform(first, (D,), jnp.float32, jnp.log(0.3), jnp.log(3.0)))
    scaling = jnp.exp(jax.random.uniform(second, shape[:-1] + (1,), jnp.float32, jnp.log(0.5), jnp.log(1.5)))
    values = jnp.clip(jax.random.normal(third, shape, jnp.float32), -4.0, 4.0) * columns * scaling
    return values.astype(jnp.bfloat16)


def draw_targets(key, part):
    first = jax.random.fold_in(key, 0)
    third = jax.random.fold_in(key, 2)
    shape = (COHORTS, CLIENTS, STEPS, STEP_TOKENS, FF)
    rising = 1.0 + 2.0 * jnp.arange(FF, dtype=jnp.float32) / FF
    jitter = jnp.exp(jax.random.uniform(first, (FF,), jnp.float32, jnp.log(0.5), jnp.log(2.0)))
    values = 0.5 * jnp.clip(jax.random.normal(third, shape, jnp.float32), -4.0, 4.0) * rising * jitter
    return values.astype(jnp.bfloat16)


def steps_of(own_key, extent, shards, least, top_value):
    loudness = 1.0
    for axis_at, parts in shards:
        draws = jax.random.uniform(jax.random.fold_in(jax.random.fold_in(own_key, 6), axis_at), (parts,), jnp.float32, least / len(shards), top_value / len(shards))
        loudness = loudness * jnp.repeat(jnp.exp(draws), extent[axis_at] // parts).reshape((-1,) + (1,) * (len(extent) - 1 - axis_at))
    return loudness


def scatter_about(stream_key, shape, deviation, limit, cuts=(), held_as=jnp.bfloat16):
    values = jax.random.normal(stream_key, shape, jnp.float32) * deviation
    if len(cuts) > 0:
        values = steps_of(stream_key, shape, cuts, -0.22, 0.18) * values
    return jnp.clip(values, min=-limit, max=limit).astype(held_as)


def setup_inputs(seed: int = 0) -> dict:
    streams_of = jax.random.split(jax.random.key(seed), 7)
    return {
        "client_tokens": draw_client_tokens(jax.random.fold_in(streams_of[6], 71), 0),
        "targets": draw_targets(jax.random.fold_in(streams_of[6], 71), 0),
        "weights": scatter_about(streams_of[2], (FF, D), 1.0, 6.0, ((0, 8),)),
        "momentum": scatter_about(streams_of[3], (FF, D), 0.3, 2.0, ((0, 8), (1, 4)), jnp.float32),
        "noise_now": scatter_about(streams_of[4], (FF, D), 1.0, 6.0, ((0, 8), (1, 4))),
        "noise_prev": scatter_about(streams_of[5], (FF, D), 1.0, 6.0, ((0, 8), (1, 4))),
    }


LOCAL_LR = 300.0
CLIP_BOUND = 32.0
NOISE_STD = 0.0004
BAND_COEF = 0.5
MOMENTUM_DECAY = 0.9
SERVER_LR = 0.5
EPSILON = 1e-06

def gelu_parts(preact):
    inner = 0.7978845608 * (preact + 0.044715 * preact * preact * preact)
    tangent = jnp.tanh(inner)
    activation = 0.5 * preact * (1.0 + tangent)
    slope = 0.5 * (1.0 + tangent) + 0.5 * preact * (1.0 - tangent * tangent) * 0.7978845608 * (1.0 + 3.0 * 0.044715 * preact * preact)
    return (activation, slope)

def local_delta(step_tokens, step_targets, weights, base_weights):
    client_delta = jnp.zeros(base_weights.shape, jnp.float32)
    current = weights
    for step_index in range(STEPS):
        token_block = step_tokens[step_index]
        preact = lax.dot_general(token_block, current, (((1,), (1,)), ((), ())), preferred_element_type=jnp.float32) * (1.0 / math.sqrt(D))
        activation, slope = gelu_parts(preact)
        error_term = ((activation - step_targets[step_index].astype(jnp.float32)) * slope).astype(jnp.bfloat16)
        gradient = lax.dot_general(error_term, token_block, (((0,), (0,)), ((), ())), preferred_element_type=jnp.float32)
        client_delta = client_delta - LOCAL_LR / (STEP_TOKENS * math.sqrt(D)) * gradient
        if step_index + 1 < STEPS:
            current = (base_weights + client_delta).astype(jnp.bfloat16)
    return client_delta

def reference(client_tokens, targets, weights, momentum, noise_now, noise_prev):
    base_weights = weights.astype(jnp.float32)
    token_list = client_tokens.reshape(COHORTS * CLIENTS, STEPS, STEP_TOKENS, D)
    target_list = targets.reshape(COHORTS * CLIENTS, STEPS, STEP_TOKENS, FF)

    def one_client(carry, pair):
        client_delta = local_delta(pair[0], pair[1], weights, base_weights)
        squared = jnp.sum(client_delta * client_delta)
        factor = jnp.minimum(1.0, CLIP_BOUND / (jnp.sqrt(squared) + EPSILON))
        return (carry + factor * client_delta, None)
    total, _ = lax.scan(one_client, jnp.zeros(base_weights.shape, jnp.float32), (token_list, target_list))
    noise = NOISE_STD * CLIP_BOUND * (noise_now.astype(jnp.float32) - BAND_COEF * noise_prev.astype(jnp.float32))
    aggregate = math.sqrt(FF * D) / (COHORTS * CLIENTS * CLIP_BOUND) * (total + noise)
    new_momentum = MOMENTUM_DECAY * momentum + aggregate
    new_weights = (base_weights + SERVER_LR * new_momentum).astype(jnp.bfloat16)
    return (new_weights, new_momentum)
```

```python
import math

import jax
import jax.numpy as jnp
from jax import lax
from jax.sharding import PartitionSpec as P

LOCAL_LR = 300.0
CLIP_BOUND = 32.0
NOISE_STD = 0.0004
BAND_COEF = 0.5
MOMENTUM_DECAY = 0.9
SERVER_LR = 0.5
EPSILON = 1e-06


def gelu_parts(preact):
    inner = 0.7978845608 * (preact + 0.044715 * preact * preact * preact)
    tangent = jnp.tanh(inner)
    activation = 0.5 * preact * (1.0 + tangent)
    slope = 0.5 * (1.0 + tangent) + 0.5 * preact * (1.0 - tangent * tangent) * 0.7978845608 * (
        1.0 + 3.0 * 0.044715 * preact * preact
    )
    return (activation, slope)


def clip_factor(squared):
    return jnp.minimum(1.0, CLIP_BOUND / (jnp.sqrt(squared) + EPSILON))


def errors_of(preact, targets):
    activation, slope = gelu_parts(preact)
    return ((activation - targets.astype(jnp.float32)) * slope).astype(jnp.bfloat16)


def client_errors(tokens, targets, weights):
    clients, steps, count, depth = tokens.shape
    rate = LOCAL_LR / (count * math.sqrt(depth))
    scale = 1.0 / math.sqrt(depth)
    flat = tokens.reshape(clients, steps * count, depth)
    products = lax.dot_general(
        flat.reshape(clients * steps * count, depth),
        weights,
        (((1,), (1,)), ((), ())),
        preferred_element_type=jnp.float32,
    ).reshape(clients, steps, count, weights.shape[0])
    gram = jnp.einsum("ksd,ktd->kst", flat, flat, preferred_element_type=jnp.float32)
    errors = []
    for step in range(steps):
        preact = products[:, step]
        if step > 0:
            earlier = jnp.concatenate(errors, axis=1).astype(jnp.float32)
            cross = gram[:, step * count : (step + 1) * count, : step * count]
            preact = preact - rate * jnp.einsum(
                "kst,ktf->ksf", cross, earlier, precision=lax.Precision.HIGHEST
            )
        errors.append(errors_of(preact * scale, targets[:, step]))
    errors = jnp.concatenate(errors, axis=1)
    error_gram = jnp.einsum("ksf,ktf->kst", errors, errors, preferred_element_type=jnp.float32)
    squared = rate * rate * jnp.maximum(jnp.sum(error_gram * gram, axis=(1, 2)), 0.0)
    return errors, squared, rate


def weighted_sum(errors, factors, tokens):
    clients, count, hidden = errors.shape
    scaled = errors.astype(jnp.float32) * factors[:, None, None]
    high = scaled.astype(jnp.bfloat16)
    low = (scaled - high.astype(jnp.float32)).astype(jnp.bfloat16)
    tokens = tokens.reshape(clients * count, -1)
    dims = (((0,), (0,)), ((), ()))
    return sum(
        lax.dot_general(
            part.reshape(clients * count, hidden), tokens, dims, preferred_element_type=jnp.float32
        )
        for part in (high, low)
    )


def body(client_tokens, targets, weights, momentum, noise_now, noise_prev):
    depth = weights.shape[1]
    clients = client_tokens.shape[1]
    round_block = lax.all_gather(client_tokens[0], "fsdp", axis=2, tiled=True)
    errors, squared, rate = client_errors(round_block, targets[0], weights)
    squared = lax.psum(squared, "fsdp")
    cohort_sum = weighted_sum(errors, -rate * clip_factor(squared), round_block)
    totals = lax.psum_scatter(cohort_sum, "cohort", scatter_dimension=1, tiled=True)
    owner_width = totals.shape[1]
    owner_start = lax.axis_index("cohort") * owner_width
    base_part = lax.dynamic_slice_in_dim(weights, owner_start, owner_width, 1).astype(jnp.float32)
    cohort_count = lax.axis_size("cohort")
    hidden_count = weights.shape[0] * lax.axis_size("fsdp")
    noise = (
        NOISE_STD
        * CLIP_BOUND
        * (noise_now.astype(jnp.float32) - BAND_COEF * noise_prev.astype(jnp.float32))
    )
    aggregate = (
        math.sqrt(hidden_count * depth) / (cohort_count * clients * CLIP_BOUND) * (totals + noise)
    )
    new_momentum = MOMENTUM_DECAY * momentum + aggregate
    new_part = (base_part + SERVER_LR * new_momentum).astype(jnp.bfloat16)
    new_weights = lax.all_gather(new_part, "cohort", axis=1, tiled=True)
    return (new_weights, new_momentum)


def solution(mesh):
    in_specs = (
        P("cohort", None, None, "fsdp", None),
        P("cohort", None, None, None, "fsdp"),
        P("fsdp", None),
        P("fsdp", "cohort"),
        P("fsdp", "cohort"),
        P("fsdp", "cohort"),
    )
    out_specs = (P("fsdp", None), P("fsdp", "cohort"))
    return jax.shard_map(body, mesh=mesh, in_specs=in_specs, out_specs=out_specs, check_vma=False)
```

```python
import math

import jax
import jax.numpy as jnp
from jax import lax
from jax.experimental import pallas as pl
from jax.experimental.pallas import tpu as pltpu
from jax.sharding import PartitionSpec as P

LOCAL_LR = 300.0
CLIP_BOUND = 32.0
NOISE_STD = 0.0004
BAND_COEF = 0.5
MOMENTUM_DECAY = 0.9
SERVER_LR = 0.5
EPSILON = 1e-06


def gelu_parts(preact):
    inner = 0.7978845608 * (preact + 0.044715 * preact * preact * preact)
    tangent = jnp.tanh(inner)
    activation = 0.5 * preact * (1.0 + tangent)
    slope = 0.5 * (1.0 + tangent) + 0.5 * preact * (1.0 - tangent * tangent) * 0.7978845608 * (
        1.0 + 3.0 * 0.044715 * preact * preact
    )
    return (activation, slope)


def clip_factor(squared):
    return jnp.minimum(1.0, CLIP_BOUND / (jnp.sqrt(squared) + EPSILON))


def errors_of(preact, targets):
    activation, slope = gelu_parts(preact)
    return ((activation - targets.astype(jnp.float32)) * slope).astype(jnp.bfloat16)


MESH = pl.DeviceIdType.MESH
ANY = pl.BlockSpec(memory_space=pl.ANY)
IN_VMEM = pl.BlockSpec(memory_space=pltpu.VMEM)
DMA = pltpu.SemaphoreType.DMA


def remote(source, target, send, receive, cohort, fsdp):
    return pltpu.make_async_remote_copy(
        src_ref=source,
        dst_ref=target,
        send_sem=send,
        recv_sem=receive,
        device_id={"cohort": cohort, "fsdp": fsdp},
        device_id_type=MESH,
    )


def signal(cohort, fsdp):
    pl.semaphore_signal(
        pltpu.get_barrier_semaphore(),
        inc=1,
        device_id={"cohort": cohort, "fsdp": fsdp},
        device_id_type=MESH,
    )


def gather_kernel(
    cohorts, shards, own_ref, all_ref, cut_ref, got, got_cut, to_up, to_down, to_pair, to_cut, kept, kept_cut
):
    c, f = lax.axis_index("cohort"), lax.axis_index("fsdp")
    rows = shards // 2
    row, side = f // 2, f % 2
    pair = f + 1 - 2 * side
    width = cut_ref.shape[-1]
    others = [(c + j) % cohorts for j in range(1, cohorts)]

    signal(c, (f + 2) % shards)
    signal(c, (f + shards - 2) % shards)
    signal(c, pair)
    for other in others:
        signal(other, f)
    pl.semaphore_wait(pltpu.get_barrier_semaphore(), cohorts + 2)

    def up(slot, source):
        return remote(source, all_ref.at[slot], to_up.at[slot], got.at[slot], c, f + 2)

    def down(slot, source):
        return remote(source, all_ref.at[slot], to_down.at[slot], got.at[slot], c, f - 2)

    def across(slot, source):
        return remote(source, all_ref.at[slot], to_pair.at[slot], got.at[slot], c, pair)

    def columns(source, owner):
        return source.at[:, pl.ds(pl.multiple_of(owner * width, 128), width)]

    def cuts(slot, source):
        copies = [
            remote(
                columns(source, other),
                cut_ref.at[c, slot],
                to_cut.at[at, slot],
                got_cut.at[c, slot],
                other,
                f,
            )
            for at, other in enumerate(others)
        ]
        own = pltpu.make_async_copy(columns(source, c), cut_ref.at[c, slot], kept_cut.at[slot])
        return copies + [own]

    def arrived(slot):
        remote(
            all_ref.at[slot], all_ref.at[slot], to_pair.at[slot], got.at[slot], c, pair
        ).wait_recv()

    def start(copies):
        for copy in copies:
            copy.start()

    keep = pltpu.make_async_copy(own_ref, all_ref.at[f], kept)

    @pl.when(row + 1 < rows)
    def _():
        up(f, own_ref).start()

    @pl.when(row > 0)
    def _():
        down(f, own_ref).start()

    across(f, own_ref).start()
    start(cuts(f, own_ref))
    keep.start()

    for step in range(1, rows + 1):

        @pl.when(row >= step)
        def _():
            slot = f - 2 * step
            arrived(slot)

            @pl.when(row + 1 < rows)
            def _():
                up(slot, all_ref.at[slot]).start()

            across(slot, all_ref.at[slot]).start()
            start(cuts(slot, all_ref.at[slot]))

        @pl.when(row + step < rows)
        def _():
            slot = f + 2 * step
            arrived(slot)

            @pl.when(row > 0)
            def _():
                down(slot, all_ref.at[slot]).start()

            across(slot, all_ref.at[slot]).start()
            start(cuts(slot, all_ref.at[slot]))

        last = step - 1

        @pl.when(row >= last)
        def _():
            slot = pair - 2 * last
            arrived(slot)
            start(cuts(slot, all_ref.at[slot]))

        if last > 0:

            @pl.when(row + last < rows)
            def _():
                slot = pair + 2 * last
                arrived(slot)
                start(cuts(slot, all_ref.at[slot]))

    keep.wait()
    for line in range(rows):
        slot = 2 * line + side

        @pl.when((row + 1 < rows) & (line <= row))
        def _():
            up(slot, own_ref).wait_send()

        @pl.when((row > 0) & (line >= row))
        def _():
            down(slot, own_ref).wait_send()

        across(slot, own_ref).wait_send()
    for slot in range(shards):
        *sent, own = cuts(slot, own_ref)
        own.wait()
        for copy in sent:
            copy.wait_send()
        for other in others:
            remote(
                cut_ref.at[other, slot],
                cut_ref.at[other, slot],
                to_pair.at[slot],
                got_cut.at[other, slot],
                other,
                f,
            ).wait_recv()


def gather_tokens(tokens, cohorts, shards):
    count, depth = tokens.shape
    return pl.pallas_call(
        lambda *refs: gather_kernel(cohorts, shards, *refs),
        name="gather_tokens",
        out_shape=(
            jax.ShapeDtypeStruct((shards, count, depth), tokens.dtype),
            jax.ShapeDtypeStruct((cohorts, shards, count, depth // cohorts), tokens.dtype),
        ),
        in_specs=[IN_VMEM],
        out_specs=(IN_VMEM, ANY),
        scratch_shapes=[
            DMA((shards,)),
            DMA((cohorts, shards)),
            DMA((shards,)),
            DMA((shards,)),
            DMA((shards,)),
            DMA((cohorts - 1, shards)),
            DMA,
            DMA((shards,)),
        ],
        compiler_params=pltpu.CompilerParams(
            collective_id=0, has_side_effects=True, vmem_limit_bytes=60 << 20
        ),
    )(tokens)


def spread_kernel(cohorts, own_ref, all_ref, got, to_far, to_pair, kept):
    c, f = lax.axis_index("cohort"), lax.axis_index("fsdp")
    pair = c + 1 - 2 * (c % 2)
    pieces = own_ref.shape[0]
    far = [(c + 2 * j) % cohorts for j in range(1, cohorts // 2)]
    keep = pltpu.make_async_copy(own_ref, all_ref.at[c], kept)
    keep.start()

    def outward(at, piece):
        return remote(
            own_ref.at[piece],
            all_ref.at[c, piece],
            to_far.at[at, piece],
            got.at[c, piece],
            far[at],
            f,
        )

    def across(slot, piece, source):
        return remote(
            source, all_ref.at[slot, piece], to_pair.at[slot, piece], got.at[slot, piece], pair, f
        )

    for piece in range(pieces):
        for at in range(len(far)):
            outward(at, piece).start()
    for piece in range(pieces):
        across(c, piece, own_ref.at[piece]).start()
    for piece in range(pieces):
        for slot in far:
            copy = across(slot, piece, all_ref.at[slot, piece])
            copy.wait_recv()
            copy.start()
    for piece in range(pieces):
        for at in range(len(far)):
            outward(at, piece).wait_send()
        for slot in [c] + far:
            across(slot, piece, own_ref.at[piece]).wait_send()
        for j in range(cohorts // 2):
            slot = (pair + 2 * j) % cohorts
            across(slot, piece, own_ref.at[piece]).wait_recv()
    keep.wait()


def greet(cohorts, c, f, others):
    signal(c + 1 - 2 * (c % 2), f)
    for j in range(1, cohorts // 2):
        signal((c + 2 * j) % cohorts, f)
    for other in others:
        signal(c, other)
    pl.semaphore_wait(pltpu.get_barrier_semaphore(), cohorts // 2 + len(others))


def blocks_kernel(cohorts, own_ref, all_ref, got, to_far, to_pair, kept):
    greet(cohorts, lax.axis_index("cohort"), lax.axis_index("fsdp"), [])
    spread_kernel(cohorts, own_ref, all_ref, got, to_far, to_pair, kept)


def spread_blocks(block, cohorts, collective_id):
    pieces = block.shape[0]
    return pl.pallas_call(
        lambda *refs: blocks_kernel(cohorts, *refs),
        name="spread_blocks",
        out_shape=jax.ShapeDtypeStruct((cohorts,) + block.shape, block.dtype),
        in_specs=[IN_VMEM],
        out_specs=ANY,
        scratch_shapes=[
            DMA((cohorts, pieces)),
            DMA((max(cohorts // 2 - 1, 1), pieces)),
            DMA((cohorts, pieces)),
            DMA,
        ],
        compiler_params=pltpu.CompilerParams(
            collective_id=collective_id, has_side_effects=True, vmem_limit_bytes=60 << 20
        ),
    )(block)


def errors_kernel(
    cohorts, shards, own_ref, part_ref, all_ref, norm_ref,
    got, to_far, to_pair, kept, parts, total, got_part, to_part, got_norm, to_norm,
):
    c, f = lax.axis_index("cohort"), lax.axis_index("fsdp")
    others = [(f + j) % shards for j in range(1, shards)]
    cohort_others = [(c + j) % cohorts for j in range(1, cohorts)]
    barrier = pltpu.get_barrier_semaphore()
    for other in others:
        signal(c, other)
    for other in cohort_others:
        signal(other, f)
    pl.semaphore_wait(barrier, len(others) + len(cohort_others))

    def part(at, source):
        return remote(part_ref, parts.at[source], to_part.at[at], got_part.at[source], c, others[at])

    def norm(at, source):
        return remote(
            total, norm_ref.at[source], to_norm.at[at], got_norm.at[source], cohort_others[at], f
        )

    for at in range(len(others)):
        part(at, f).start()
    parts[pl.ds(f, 1)] = part_ref[...][None]
    for at, other in enumerate(others):
        part(at, other).wait_recv()
    summed = parts[0]
    for at in range(1, shards):
        summed = summed + parts[at]
    total[...] = summed
    norm_ref[pl.ds(c, 1)] = summed[None]
    for at in range(len(cohort_others)):
        norm(at, c).start()
    spread_kernel(cohorts, own_ref, all_ref, got, to_far, to_pair, kept)
    for at, other in enumerate(cohort_others):
        norm(at, other).wait_recv()
        norm(at, c).wait_send()
    for at in range(len(others)):
        part(at, f).wait_send()


def spread_errors(errors, squared, cohorts, shards):
    pieces = errors.shape[0]
    tile = jnp.broadcast_to(squared[:, None], (squared.shape[0], 128))
    return pl.pallas_call(
        lambda *refs: errors_kernel(cohorts, shards, *refs),
        name="spread_errors",
        out_shape=(
            jax.ShapeDtypeStruct((cohorts,) + errors.shape, errors.dtype),
            jax.ShapeDtypeStruct((cohorts,) + tile.shape, tile.dtype),
        ),
        in_specs=[IN_VMEM, IN_VMEM],
        out_specs=(ANY, IN_VMEM),
        scratch_shapes=[
            DMA((cohorts, pieces)),
            DMA((max(cohorts // 2 - 1, 1), pieces)),
            DMA((cohorts, pieces)),
            DMA,
            pltpu.VMEM((shards,) + tile.shape, tile.dtype),
            pltpu.VMEM(tile.shape, tile.dtype),
            DMA((shards,)),
            DMA((shards,)),
            DMA((cohorts,)),
            DMA((cohorts,)),
        ],
        compiler_params=pltpu.CompilerParams(
            collective_id=1, has_side_effects=True, vmem_limit_bytes=60 << 20
        ),
    )(errors, tile)


def client_errors(tokens, targets, weights):
    clients, steps, count, depth = tokens.shape
    rate = LOCAL_LR / (count * math.sqrt(depth))
    scale = 1.0 / math.sqrt(depth)
    flat = tokens.reshape(clients, steps * count, depth)
    products = lax.dot_general(
        flat.reshape(clients * steps * count, depth),
        weights,
        (((1,), (1,)), ((), ())),
        preferred_element_type=jnp.float32,
    ).reshape(clients, steps, count, weights.shape[0])
    gram = jnp.einsum("ksd,ktd->kst", flat, flat, preferred_element_type=jnp.float32)
    errors = []
    for step in range(steps):
        preact = products[:, step]
        if step > 0:
            earlier = jnp.concatenate(errors, axis=1).astype(jnp.float32)
            cross = gram[:, step * count : (step + 1) * count, : step * count]
            preact = preact - rate * jnp.einsum(
                "kst,ktf->ksf", cross, earlier, precision=lax.Precision.HIGHEST
            )
        errors.append(errors_of(preact * scale, targets[:, step]))
    errors = jnp.concatenate(errors, axis=1)
    error_gram = jnp.einsum("ksf,ktf->kst", errors, errors, preferred_element_type=jnp.float32)
    squared = rate * rate * jnp.maximum(jnp.sum(error_gram * gram, axis=(1, 2)), 0.0)
    return errors, squared, rate


def weighted_sum(errors, factors, tokens):
    hidden, width = errors.shape[-1], tokens.shape[-1]
    scaled = errors.astype(jnp.float32) * factors
    high = scaled.astype(jnp.bfloat16)
    low = (scaled - high.astype(jnp.float32)).astype(jnp.bfloat16)
    tokens = tokens.reshape(-1, width)
    dims = (((0,), (0,)), ((), ()))
    return sum(
        lax.dot_general(
            part.reshape(-1, hidden), tokens, dims, preferred_element_type=jnp.float32
        )
        for part in (high, low)
    )


def factor_body(client_tokens, targets, weights, momentum, noise_now, noise_prev):
    cohorts, shards = lax.axis_size("cohort"), lax.axis_size("fsdp")
    hidden, depth = weights.shape
    _, clients, steps, count, _ = client_tokens.shape
    gathered, columns = gather_tokens(client_tokens.reshape(-1, depth), cohorts, shards)
    tokens = gathered.reshape(shards, clients, steps, count, depth)
    tokens = tokens.transpose(1, 2, 0, 3, 4).reshape(clients, steps, shards * count, depth)
    errors, squared, rate = client_errors(tokens, targets[0], weights)
    errors = errors.reshape(clients, steps, shards, count, hidden).transpose(2, 0, 1, 3, 4)
    errors, squared = spread_errors(errors.reshape(shards, -1, hidden), squared, cohorts, shards)
    factors = -rate * clip_factor(squared[:, :, 0])
    errors = errors.reshape(cohorts, shards, clients, steps * count, hidden)
    totals = weighted_sum(errors, factors[:, None, :, None, None], columns)
    owner_width = totals.shape[1]
    owner_start = lax.axis_index("cohort") * owner_width
    base_part = lax.dynamic_slice_in_dim(weights, owner_start, owner_width, 1).astype(jnp.float32)
    hidden_count = hidden * shards
    noise = (
        NOISE_STD
        * CLIP_BOUND
        * (noise_now.astype(jnp.float32) - BAND_COEF * noise_prev.astype(jnp.float32))
    )
    aggregate = (
        math.sqrt(hidden_count * depth) / (cohorts * clients * CLIP_BOUND) * (totals + noise)
    )
    new_momentum = MOMENTUM_DECAY * momentum + aggregate
    new_part = (base_part + SERVER_LR * new_momentum).astype(jnp.bfloat16)
    pieces = math.gcd(hidden // 16, 8)
    new_part = new_part.reshape(pieces, hidden // pieces, owner_width)
    blocks = spread_blocks(new_part, cohorts, 2).reshape(cohorts, hidden, owner_width)
    new_weights = blocks.transpose(1, 0, 2).reshape(hidden, depth)
    return (new_weights, new_momentum)


def sum_body(client_tokens, targets, weights, momentum, noise_now, noise_prev):
    depth = weights.shape[1]
    clients = client_tokens.shape[1]
    round_block = lax.all_gather(client_tokens[0], "fsdp", axis=2, tiled=True)
    errors, squared, rate = client_errors(round_block, targets[0], weights)
    squared = lax.psum(squared, "fsdp")
    cohort_sum = weighted_sum(
        errors, (-rate * clip_factor(squared))[:, None, None], round_block
    )
    totals = lax.psum_scatter(cohort_sum, "cohort", scatter_dimension=1, tiled=True)
    owner_width = totals.shape[1]
    owner_start = lax.axis_index("cohort") * owner_width
    base_part = lax.dynamic_slice_in_dim(weights, owner_start, owner_width, 1).astype(jnp.float32)
    cohort_count = lax.axis_size("cohort")
    hidden_count = weights.shape[0] * lax.axis_size("fsdp")
    noise = (
        NOISE_STD
        * CLIP_BOUND
        * (noise_now.astype(jnp.float32) - BAND_COEF * noise_prev.astype(jnp.float32))
    )
    aggregate = (
        math.sqrt(hidden_count * depth) / (cohort_count * clients * CLIP_BOUND) * (totals + noise)
    )
    new_momentum = MOMENTUM_DECAY * momentum + aggregate
    new_part = (base_part + SERVER_LR * new_momentum).astype(jnp.bfloat16)
    new_weights = lax.all_gather(new_part, "cohort", axis=1, tiled=True)
    return (new_weights, new_momentum)


def body(client_tokens, *others):
    _, clients, steps, count, _ = client_tokens.shape
    hidden = others[1].shape[0]
    rank = clients * steps * count * lax.axis_size("fsdp")
    few = rank <= hidden and lax.axis_size("cohort") % 2 == 0 and lax.axis_size("fsdp") % 2 == 0
    return (factor_body if few else sum_body)(client_tokens, *others)


def solution(mesh):
    in_specs = (
        P("cohort", None, None, "fsdp", None),
        P("cohort", None, None, None, "fsdp"),
        P("fsdp", None),
        P("fsdp", "cohort"),
        P("fsdp", "cohort"),
        P("fsdp", "cohort"),
    )
    out_specs = (P("fsdp", None), P("fsdp", "cohort"))
    return jax.shard_map(body, mesh=mesh, in_specs=in_specs, out_specs=out_specs, check_vma=False)
```

```python
import math

import jax
import jax.numpy as jnp
from jax import lax
from jax.experimental import pallas as pl
from jax.experimental.pallas import tpu as pltpu
from jax.sharding import PartitionSpec as P

LOCAL_LR = 300.0
CLIP_BOUND = 32.0
NOISE_STD = 0.0004
BAND_COEF = 0.5
MOMENTUM_DECAY = 0.9
SERVER_LR = 0.5
EPSILON = 1e-06


def gelu_parts(preact):
    inner = 0.7978845608 * (preact + 0.044715 * preact * preact * preact)
    tangent = jnp.tanh(inner)
    activation = 0.5 * preact * (1.0 + tangent)
    slope = 0.5 * (1.0 + tangent) + 0.5 * preact * (1.0 - tangent * tangent) * 0.7978845608 * (
        1.0 + 3.0 * 0.044715 * preact * preact
    )
    return (activation, slope)


def clip_factor(squared):
    return jnp.minimum(1.0, CLIP_BOUND / (jnp.sqrt(squared) + EPSILON))


def errors_of(preact, targets):
    activation, slope = gelu_parts(preact)
    return ((activation - targets.astype(jnp.float32)) * slope).astype(jnp.bfloat16)


MESH = pl.DeviceIdType.MESH
ANY = pl.BlockSpec(memory_space=pl.ANY)
IN_VMEM = pl.BlockSpec(memory_space=pltpu.VMEM)
DMA = pltpu.SemaphoreType.DMA


def remote(source, target, send, receive, cohort, fsdp):
    return pltpu.make_async_remote_copy(
        src_ref=source,
        dst_ref=target,
        send_sem=send,
        recv_sem=receive,
        device_id={"cohort": cohort, "fsdp": fsdp},
        device_id_type=MESH,
    )


def signal(cohort, fsdp):
    pl.semaphore_signal(
        pltpu.get_barrier_semaphore(),
        inc=1,
        device_id={"cohort": cohort, "fsdp": fsdp},
        device_id_type=MESH,
    )


def gather_kernel(
    cohorts, shards, own_ref, all_ref, cut_ref, got, got_cut, to_up, to_down, to_pair, to_cut, kept, kept_cut
):
    c, f = lax.axis_index("cohort"), lax.axis_index("fsdp")
    rows = shards // 2
    row, side = f // 2, f % 2
    pair = f + 1 - 2 * side
    width = cut_ref.shape[-1]
    others = [(c + j) % cohorts for j in range(1, cohorts)]

    signal(c, (f + 2) % shards)
    signal(c, (f + shards - 2) % shards)
    signal(c, pair)
    for other in others:
        signal(other, f)
    pl.semaphore_wait(pltpu.get_barrier_semaphore(), cohorts + 2)

    pieces = own_ref.shape[0]

    def up(slot, piece, source):
        return remote(
            source, all_ref.at[slot, piece], to_up.at[slot, piece], got.at[slot, piece], c, f + 2
        )

    def down(slot, piece, source):
        return remote(
            source, all_ref.at[slot, piece], to_down.at[slot, piece], got.at[slot, piece], c, f - 2
        )

    def across(slot, piece, source):
        return remote(
            source, all_ref.at[slot, piece], to_pair.at[slot, piece], got.at[slot, piece], c, pair
        )

    def columns(source, owner):
        return source.at[:, pl.ds(pl.multiple_of(owner * width, 128), width)]

    def cuts(slot, piece, source):
        copies = [
            remote(
                columns(source, other),
                cut_ref.at[c, slot, piece],
                to_cut.at[at, slot, piece],
                got_cut.at[c, slot, piece],
                other,
                f,
            )
            for at, other in enumerate(others)
        ]
        own = pltpu.make_async_copy(
            columns(source, c), cut_ref.at[c, slot, piece], kept_cut.at[slot, piece]
        )
        return copies + [own]

    def arrived(slot, piece):
        across(slot, piece, own_ref.at[0]).wait_recv()

    def start(copies):
        for copy in copies:
            copy.start()

    keep = pltpu.make_async_copy(own_ref, all_ref.at[f], kept)
    for piece in range(pieces):

        @pl.when(row + 1 < rows)
        def _():
            up(f, piece, own_ref.at[piece]).start()

        @pl.when(row > 0)
        def _():
            down(f, piece, own_ref.at[piece]).start()

        across(f, piece, own_ref.at[piece]).start()
        start(cuts(f, piece, own_ref.at[piece]))
    keep.start()

    for step in range(1, rows + 1):
        last = step - 1
        for piece in range(pieces):

            @pl.when(row >= step)
            def _():
                slot = f - 2 * step
                arrived(slot, piece)

                @pl.when(row + 1 < rows)
                def _():
                    up(slot, piece, all_ref.at[slot, piece]).start()

                across(slot, piece, all_ref.at[slot, piece]).start()
                start(cuts(slot, piece, all_ref.at[slot, piece]))

            @pl.when(row + step < rows)
            def _():
                slot = f + 2 * step
                arrived(slot, piece)

                @pl.when(row > 0)
                def _():
                    down(slot, piece, all_ref.at[slot, piece]).start()

                across(slot, piece, all_ref.at[slot, piece]).start()
                start(cuts(slot, piece, all_ref.at[slot, piece]))

            @pl.when(row >= last)
            def _():
                slot = pair - 2 * last
                arrived(slot, piece)
                start(cuts(slot, piece, all_ref.at[slot, piece]))

            if last > 0:

                @pl.when(row + last < rows)
                def _():
                    slot = pair + 2 * last
                    arrived(slot, piece)
                    start(cuts(slot, piece, all_ref.at[slot, piece]))

    keep.wait()
    for piece in range(pieces):
        source = own_ref.at[piece]
        for line in range(rows):
            slot = 2 * line + side

            @pl.when((row + 1 < rows) & (line <= row))
            def _():
                up(slot, piece, source).wait_send()

            @pl.when((row > 0) & (line >= row))
            def _():
                down(slot, piece, source).wait_send()

            across(slot, piece, source).wait_send()
        for slot in range(shards):
            *sent, own = cuts(slot, piece, source)
            own.wait()
            for copy in sent:
                copy.wait_send()
            for other in others:
                remote(
                    columns(source, c),
                    cut_ref.at[other, slot, piece],
                    to_pair.at[slot, piece],
                    got_cut.at[other, slot, piece],
                    other,
                    f,
                ).wait_recv()


def gather_tokens(tokens, cohorts, shards):
    pieces, count, depth = tokens.shape
    return pl.pallas_call(
        lambda *refs: gather_kernel(cohorts, shards, *refs),
        name="gather_tokens",
        out_shape=(
            jax.ShapeDtypeStruct((shards, pieces, count, depth), tokens.dtype),
            jax.ShapeDtypeStruct((cohorts, shards, pieces, count, depth // cohorts), tokens.dtype),
        ),
        in_specs=[IN_VMEM],
        out_specs=(IN_VMEM, ANY),
        scratch_shapes=[
            DMA((shards, pieces)),
            DMA((cohorts, shards, pieces)),
            DMA((shards, pieces)),
            DMA((shards, pieces)),
            DMA((shards, pieces)),
            DMA((cohorts - 1, shards, pieces)),
            DMA,
            DMA((shards, pieces)),
        ],
        compiler_params=pltpu.CompilerParams(
            collective_id=0, has_side_effects=True, vmem_limit_bytes=60 << 20
        ),
    )(tokens)


def spread_kernel(cohorts, own_ref, all_ref, got, to_far, to_pair, kept, meanwhile=None):
    c, f = lax.axis_index("cohort"), lax.axis_index("fsdp")
    pair = c + 1 - 2 * (c % 2)
    pieces = own_ref.shape[0]
    far = [(c + 2 * j) % cohorts for j in range(1, cohorts // 2)]
    keep = pltpu.make_async_copy(own_ref, all_ref.at[c], kept)
    keep.start()

    def outward(at, piece):
        return remote(
            own_ref.at[piece],
            all_ref.at[c, piece],
            to_far.at[at, piece],
            got.at[c, piece],
            far[at],
            f,
        )

    def across(slot, piece, source):
        return remote(
            source, all_ref.at[slot, piece], to_pair.at[slot, piece], got.at[slot, piece], pair, f
        )

    for piece in range(pieces):
        for at in range(len(far)):
            outward(at, piece).start()
    for piece in range(pieces):
        across(c, piece, own_ref.at[piece]).start()
    if meanwhile is not None:
        meanwhile()
    for piece in range(pieces):
        for slot in far:
            copy = across(slot, piece, all_ref.at[slot, piece])
            copy.wait_recv()
            copy.start()
    for piece in range(pieces):
        for at in range(len(far)):
            outward(at, piece).wait_send()
        for slot in [c] + far:
            across(slot, piece, own_ref.at[piece]).wait_send()
        for j in range(cohorts // 2):
            slot = (pair + 2 * j) % cohorts
            across(slot, piece, own_ref.at[piece]).wait_recv()
    keep.wait()


def greet(cohorts, c, f, others):
    signal(c + 1 - 2 * (c % 2), f)
    for j in range(1, cohorts // 2):
        signal((c + 2 * j) % cohorts, f)
    for other in others:
        signal(c, other)
    pl.semaphore_wait(pltpu.get_barrier_semaphore(), cohorts // 2 + len(others))


def blocks_kernel(cohorts, own_ref, all_ref, got, to_far, to_pair, kept):
    greet(cohorts, lax.axis_index("cohort"), lax.axis_index("fsdp"), [])
    spread_kernel(cohorts, own_ref, all_ref, got, to_far, to_pair, kept)


def spread_blocks(block, cohorts, collective_id):
    pieces = block.shape[0]
    return pl.pallas_call(
        lambda *refs: blocks_kernel(cohorts, *refs),
        name="spread_blocks",
        out_shape=jax.ShapeDtypeStruct((cohorts,) + block.shape, block.dtype),
        in_specs=[IN_VMEM],
        out_specs=ANY,
        scratch_shapes=[
            DMA((cohorts, pieces)),
            DMA((max(cohorts // 2 - 1, 1), pieces)),
            DMA((cohorts, pieces)),
            DMA,
        ],
        compiler_params=pltpu.CompilerParams(
            collective_id=collective_id, has_side_effects=True, vmem_limit_bytes=60 << 20
        ),
    )(block)


def errors_kernel(
    cohorts, shards, own_ref, part_ref, all_ref, norm_ref,
    got, to_far, to_pair, kept, parts, total, got_part, to_part, got_norm, to_norm,
):
    c, f = lax.axis_index("cohort"), lax.axis_index("fsdp")
    others = [(f + j) % shards for j in range(1, shards)]
    cohort_others = [(c + j) % cohorts for j in range(1, cohorts)]
    barrier = pltpu.get_barrier_semaphore()
    for other in others:
        signal(c, other)
    for other in cohort_others:
        signal(other, f)
    pl.semaphore_wait(barrier, len(others) + len(cohort_others))

    def part(at, source):
        return remote(part_ref, parts.at[source], to_part.at[at], got_part.at[source], c, others[at])

    def norm(at, source):
        return remote(
            total, norm_ref.at[source], to_norm.at[at], got_norm.at[source], cohort_others[at], f
        )

    def sum_norms():
        parts[pl.ds(f, 1)] = part_ref[...][None]
        for at, other in enumerate(others):
            part(at, other).wait_recv()
        summed = parts[0]
        for at in range(1, shards):
            summed = summed + parts[at]
        total[...] = summed
        norm_ref[pl.ds(c, 1)] = summed[None]
        for at in range(len(cohort_others)):
            norm(at, c).start()

    for at in range(len(others)):
        part(at, f).start()
    spread_kernel(cohorts, own_ref, all_ref, got, to_far, to_pair, kept, sum_norms)
    for at, other in enumerate(cohort_others):
        norm(at, other).wait_recv()
        norm(at, c).wait_send()
    for at in range(len(others)):
        part(at, f).wait_send()


def spread_errors(errors, squared, cohorts, shards):
    pieces = errors.shape[0]
    tile = jnp.broadcast_to(squared[:, None], (squared.shape[0], 128))
    return pl.pallas_call(
        lambda *refs: errors_kernel(cohorts, shards, *refs),
        name="spread_errors",
        out_shape=(
            jax.ShapeDtypeStruct((cohorts,) + errors.shape, errors.dtype),
            jax.ShapeDtypeStruct((cohorts,) + tile.shape, tile.dtype),
        ),
        in_specs=[IN_VMEM, IN_VMEM],
        out_specs=(ANY, IN_VMEM),
        scratch_shapes=[
            DMA((cohorts, pieces)),
            DMA((max(cohorts // 2 - 1, 1), pieces)),
            DMA((cohorts, pieces)),
            DMA,
            pltpu.VMEM((shards,) + tile.shape, tile.dtype),
            pltpu.VMEM(tile.shape, tile.dtype),
            DMA((shards,)),
            DMA((shards,)),
            DMA((cohorts,)),
            DMA((cohorts,)),
        ],
        compiler_params=pltpu.CompilerParams(
            collective_id=1, has_side_effects=True, vmem_limit_bytes=60 << 20
        ),
    )(errors, tile)


def client_errors(tokens, products, targets):
    clients, steps, count, depth = tokens.shape
    rate = LOCAL_LR / (count * math.sqrt(depth))
    scale = 1.0 / math.sqrt(depth)
    flat = tokens.reshape(clients, steps * count, depth)
    gram = jnp.einsum("ksd,ktd->kst", flat, flat, preferred_element_type=jnp.float32)
    errors = []
    for step in range(steps):
        preact = products[:, step]
        if step > 0:
            earlier = jnp.concatenate(errors, axis=1).astype(jnp.float32)
            cross = gram[:, step * count : (step + 1) * count, : step * count]
            preact = preact - rate * jnp.einsum(
                "kst,ktf->ksf", cross, earlier, precision=lax.Precision.HIGHEST
            )
        errors.append(errors_of(preact * scale, targets[:, step]))
    errors = jnp.concatenate(errors, axis=1)
    error_gram = jnp.einsum("ksf,ktf->kst", errors, errors, preferred_element_type=jnp.float32)
    squared = rate * rate * jnp.maximum(jnp.sum(error_gram * gram, axis=(1, 2)), 0.0)
    return errors, squared, rate


def weighted_sum(errors, factors, tokens):
    hidden, width = errors.shape[-1], tokens.shape[-1]
    scaled = errors.astype(jnp.float32) * factors
    high = scaled.astype(jnp.bfloat16)
    low = (scaled - high.astype(jnp.float32)).astype(jnp.bfloat16)
    tokens = tokens.reshape(-1, width)
    dims = (((0,), (0,)), ((), ()))
    return sum(
        lax.dot_general(
            part.reshape(-1, hidden), tokens, dims, preferred_element_type=jnp.float32
        )
        for part in (high, low)
    )


def products_of(tokens, weights):
    return lax.dot_general(
        tokens, weights, (((1,), (1,)), ((), ())), preferred_element_type=jnp.float32
    )


def factor_body(client_tokens, targets, weights, momentum, noise_now, noise_prev):
    cohorts, shards = lax.axis_size("cohort"), lax.axis_size("fsdp")
    hidden, depth = weights.shape
    _, clients, steps, count, _ = client_tokens.shape
    pieces = max(clients * steps * count // 16, 1)
    gathered, columns = gather_tokens(
        client_tokens.reshape(pieces, -1, depth), cohorts, shards
    )
    products = products_of(gathered.reshape(-1, depth), weights)
    products = products.reshape(shards, clients, steps, count, hidden)
    products = products.transpose(1, 2, 0, 3, 4).reshape(clients, steps, shards * count, hidden)
    tokens = gathered.reshape(shards, clients, steps, count, depth)
    tokens = tokens.transpose(1, 2, 0, 3, 4).reshape(clients, steps, shards * count, depth)
    errors, squared, rate = client_errors(tokens, products, targets[0])
    errors = errors.reshape(clients, steps, shards, count, hidden).transpose(2, 0, 1, 3, 4)
    errors, squared = spread_errors(errors.reshape(shards, -1, hidden), squared, cohorts, shards)
    factors = -rate * clip_factor(squared[:, :, 0])
    errors = errors.reshape(cohorts, shards, clients, steps * count, hidden)
    totals = weighted_sum(errors, factors[:, None, :, None, None], columns)
    owner_width = totals.shape[1]
    owner_start = lax.axis_index("cohort") * owner_width
    base_part = lax.dynamic_slice_in_dim(weights, owner_start, owner_width, 1).astype(jnp.float32)
    hidden_count = hidden * shards
    noise = (
        NOISE_STD
        * CLIP_BOUND
        * (noise_now.astype(jnp.float32) - BAND_COEF * noise_prev.astype(jnp.float32))
    )
    aggregate = (
        math.sqrt(hidden_count * depth) / (cohorts * clients * CLIP_BOUND) * (totals + noise)
    )
    new_momentum = MOMENTUM_DECAY * momentum + aggregate
    new_part = (base_part + SERVER_LR * new_momentum).astype(jnp.bfloat16)
    pieces = math.gcd(hidden // 16, 8)
    new_part = new_part.reshape(pieces, hidden // pieces, owner_width)
    blocks = spread_blocks(new_part, cohorts, 2).reshape(cohorts, hidden, owner_width)
    new_weights = blocks.transpose(1, 0, 2).reshape(hidden, depth)
    return (new_weights, new_momentum)


def sum_body(client_tokens, targets, weights, momentum, noise_now, noise_prev):
    depth = weights.shape[1]
    clients = client_tokens.shape[1]
    round_block = lax.all_gather(client_tokens[0], "fsdp", axis=2, tiled=True)
    products = products_of(round_block.reshape(-1, depth), weights)
    products = products.reshape(round_block.shape[:3] + weights.shape[:1])
    errors, squared, rate = client_errors(round_block, products, targets[0])
    squared = lax.psum(squared, "fsdp")
    cohort_sum = weighted_sum(
        errors, (-rate * clip_factor(squared))[:, None, None], round_block
    )
    totals = lax.psum_scatter(cohort_sum, "cohort", scatter_dimension=1, tiled=True)
    owner_width = totals.shape[1]
    owner_start = lax.axis_index("cohort") * owner_width
    base_part = lax.dynamic_slice_in_dim(weights, owner_start, owner_width, 1).astype(jnp.float32)
    cohort_count = lax.axis_size("cohort")
    hidden_count = weights.shape[0] * lax.axis_size("fsdp")
    noise = (
        NOISE_STD
        * CLIP_BOUND
        * (noise_now.astype(jnp.float32) - BAND_COEF * noise_prev.astype(jnp.float32))
    )
    aggregate = (
        math.sqrt(hidden_count * depth) / (cohort_count * clients * CLIP_BOUND) * (totals + noise)
    )
    new_momentum = MOMENTUM_DECAY * momentum + aggregate
    new_part = (base_part + SERVER_LR * new_momentum).astype(jnp.bfloat16)
    new_weights = lax.all_gather(new_part, "cohort", axis=1, tiled=True)
    return (new_weights, new_momentum)


def body(client_tokens, *others):
    _, clients, steps, count, _ = client_tokens.shape
    hidden = others[1].shape[0]
    rank = clients * steps * count * lax.axis_size("fsdp")
    few = rank <= hidden and lax.axis_size("cohort") % 2 == 0 and lax.axis_size("fsdp") % 2 == 0
    return (factor_body if few else sum_body)(client_tokens, *others)


def solution(mesh):
    in_specs = (
        P("cohort", None, None, "fsdp", None),
        P("cohort", None, None, None, "fsdp"),
        P("fsdp", None),
        P("fsdp", "cohort"),
        P("fsdp", "cohort"),
        P("fsdp", "cohort"),
    )
    out_specs = (P("fsdp", None), P("fsdp", "cohort"))
    return jax.shard_map(body, mesh=mesh, in_specs=in_specs, out_specs=out_specs, check_vma=False)
```

```python
import math

import jax
import jax.numpy as jnp
from jax import lax
from jax.experimental import pallas as pl
from jax.experimental.pallas import tpu as pltpu
from jax.sharding import PartitionSpec as P

LOCAL_LR = 300.0
CLIP_BOUND = 32.0
NOISE_STD = 0.0004
BAND_COEF = 0.5
MOMENTUM_DECAY = 0.9
SERVER_LR = 0.5
EPSILON = 1e-06


def gelu_parts(preact):
    inner = 0.7978845608 * (preact + 0.044715 * preact * preact * preact)
    tangent = jnp.tanh(inner)
    activation = 0.5 * preact * (1.0 + tangent)
    slope = 0.5 * (1.0 + tangent) + 0.5 * preact * (1.0 - tangent * tangent) * 0.7978845608 * (
        1.0 + 3.0 * 0.044715 * preact * preact
    )
    return (activation, slope)


def clip_factor(squared):
    return jnp.minimum(1.0, CLIP_BOUND / (jnp.sqrt(squared) + EPSILON))


def errors_of(preact, targets):
    activation, slope = gelu_parts(preact)
    return ((activation - targets.astype(jnp.float32)) * slope).astype(jnp.bfloat16)


MESH = pl.DeviceIdType.MESH
ANY = pl.BlockSpec(memory_space=pl.ANY)
IN_VMEM = pl.BlockSpec(memory_space=pltpu.VMEM)
DMA = pltpu.SemaphoreType.DMA


def remote(source, target, send, receive, cohort, fsdp):
    return pltpu.make_async_remote_copy(
        src_ref=source,
        dst_ref=target,
        send_sem=send,
        recv_sem=receive,
        device_id={"cohort": cohort, "fsdp": fsdp},
        device_id_type=MESH,
    )


def signal(cohort, fsdp):
    pl.semaphore_signal(
        pltpu.get_barrier_semaphore(),
        inc=1,
        device_id={"cohort": cohort, "fsdp": fsdp},
        device_id_type=MESH,
    )


def gather_kernel(
    cohorts, shards, own_ref, all_ref, cut_ref, got, got_cut, to_up, to_down, to_pair, to_cut, kept, kept_cut
):
    c, f = lax.axis_index("cohort"), lax.axis_index("fsdp")
    rows = shards // 2
    row, side = f // 2, f % 2
    pair = f + 1 - 2 * side
    width = cut_ref.shape[-1]
    others = [(c + j) % cohorts for j in range(1, cohorts)]

    signal(c, (f + 2) % shards)
    signal(c, (f + shards - 2) % shards)
    signal(c, pair)
    for other in others:
        signal(other, f)
    pl.semaphore_wait(pltpu.get_barrier_semaphore(), cohorts + 2)

    pieces = own_ref.shape[0]

    def up(slot, piece, source):
        return remote(
            source, all_ref.at[slot, piece], to_up.at[slot, piece], got.at[slot, piece], c, f + 2
        )

    def down(slot, piece, source):
        return remote(
            source, all_ref.at[slot, piece], to_down.at[slot, piece], got.at[slot, piece], c, f - 2
        )

    def across(slot, piece, source):
        return remote(
            source, all_ref.at[slot, piece], to_pair.at[slot, piece], got.at[slot, piece], c, pair
        )

    def columns(source, owner):
        return source.at[:, pl.ds(pl.multiple_of(owner * width, 128), width)]

    def cuts(slot, piece, source):
        copies = [
            remote(
                columns(source, other),
                cut_ref.at[c, slot, piece],
                to_cut.at[at, slot, piece],
                got_cut.at[c, slot, piece],
                other,
                f,
            )
            for at, other in enumerate(others)
        ]
        own = pltpu.make_async_copy(
            columns(source, c), cut_ref.at[c, slot, piece], kept_cut.at[slot, piece]
        )
        return copies + [own]

    def arrived(slot, piece):
        across(slot, piece, own_ref.at[0]).wait_recv()

    def start(copies):
        for copy in copies:
            copy.start()

    keep = pltpu.make_async_copy(own_ref, all_ref.at[f], kept)
    for piece in range(pieces):

        @pl.when(row + 1 < rows)
        def _():
            up(f, piece, own_ref.at[piece]).start()

        @pl.when(row > 0)
        def _():
            down(f, piece, own_ref.at[piece]).start()

        across(f, piece, own_ref.at[piece]).start()
        start(cuts(f, piece, own_ref.at[piece]))
    keep.start()

    for step in range(1, rows + 1):
        last = step - 1
        for piece in range(pieces):

            @pl.when(row >= step)
            def _():
                slot = f - 2 * step
                arrived(slot, piece)

                @pl.when(row + 1 < rows)
                def _():
                    up(slot, piece, all_ref.at[slot, piece]).start()

                across(slot, piece, all_ref.at[slot, piece]).start()
                start(cuts(slot, piece, all_ref.at[slot, piece]))

            @pl.when(row + step < rows)
            def _():
                slot = f + 2 * step
                arrived(slot, piece)

                @pl.when(row > 0)
                def _():
                    down(slot, piece, all_ref.at[slot, piece]).start()

                across(slot, piece, all_ref.at[slot, piece]).start()
                start(cuts(slot, piece, all_ref.at[slot, piece]))

            @pl.when(row >= last)
            def _():
                slot = pair - 2 * last
                arrived(slot, piece)
                start(cuts(slot, piece, all_ref.at[slot, piece]))

            if last > 0:

                @pl.when(row + last < rows)
                def _():
                    slot = pair + 2 * last
                    arrived(slot, piece)
                    start(cuts(slot, piece, all_ref.at[slot, piece]))

    keep.wait()
    for piece in range(pieces):
        source = own_ref.at[piece]
        for line in range(rows):
            slot = 2 * line + side

            @pl.when((row + 1 < rows) & (line <= row))
            def _():
                up(slot, piece, source).wait_send()

            @pl.when((row > 0) & (line >= row))
            def _():
                down(slot, piece, source).wait_send()

            across(slot, piece, source).wait_send()
        for slot in range(shards):
            *sent, own = cuts(slot, piece, source)
            own.wait()
            for copy in sent:
                copy.wait_send()
            for other in others:
                remote(
                    columns(source, c),
                    cut_ref.at[other, slot, piece],
                    to_pair.at[slot, piece],
                    got_cut.at[other, slot, piece],
                    other,
                    f,
                ).wait_recv()


def gather_tokens(tokens, cohorts, shards):
    pieces, count, depth = tokens.shape
    return pl.pallas_call(
        lambda *refs: gather_kernel(cohorts, shards, *refs),
        name="gather_tokens",
        out_shape=(
            jax.ShapeDtypeStruct((shards, pieces, count, depth), tokens.dtype),
            jax.ShapeDtypeStruct((cohorts, shards, pieces, count, depth // cohorts), tokens.dtype),
        ),
        in_specs=[IN_VMEM],
        out_specs=(IN_VMEM, ANY),
        scratch_shapes=[
            DMA((shards, pieces)),
            DMA((cohorts, shards, pieces)),
            DMA((shards, pieces)),
            DMA((shards, pieces)),
            DMA((shards, pieces)),
            DMA((cohorts - 1, shards, pieces)),
            DMA,
            DMA((shards, pieces)),
        ],
        compiler_params=pltpu.CompilerParams(
            collective_id=0, has_side_effects=True, vmem_limit_bytes=60 << 20
        ),
    )(tokens)


def spread_kernel(cohorts, own_ref, all_ref, got, to_far, to_pair, kept, meanwhile=None, produce=None):
    c, f = lax.axis_index("cohort"), lax.axis_index("fsdp")
    pair = c + 1 - 2 * (c % 2)
    pieces = own_ref.shape[0]
    far = [(c + 2 * j) % cohorts for j in range(1, cohorts // 2)]
    keep = pltpu.make_async_copy(own_ref, all_ref.at[c], kept)
    if produce is None:
        keep.start()

    def outward(at, piece):
        return remote(
            own_ref.at[piece],
            all_ref.at[c, piece],
            to_far.at[at, piece],
            got.at[c, piece],
            far[at],
            f,
        )

    def across(slot, piece, source):
        return remote(
            source, all_ref.at[slot, piece], to_pair.at[slot, piece], got.at[slot, piece], pair, f
        )

    def send(piece):
        if produce is not None:
            produce(piece)
        for at in range(len(far)):
            outward(at, piece).start()
        across(c, piece, own_ref.at[piece]).start()

    if produce is None:
        for piece in range(pieces):
            send(piece)
    else:
        pl.loop(0, pieces)(send)
        keep.start()
    if meanwhile is not None:
        meanwhile()
    for piece in range(pieces):
        for slot in far:
            copy = across(slot, piece, all_ref.at[slot, piece])
            copy.wait_recv()
            copy.start()
    for piece in range(pieces):
        for at in range(len(far)):
            outward(at, piece).wait_send()
        for slot in [c] + far:
            across(slot, piece, own_ref.at[piece]).wait_send()
        for j in range(cohorts // 2):
            slot = (pair + 2 * j) % cohorts
            across(slot, piece, own_ref.at[piece]).wait_recv()
    keep.wait()


def greet(cohorts, c, f, others):
    signal(c + 1 - 2 * (c % 2), f)
    for j in range(1, cohorts // 2):
        signal((c + 2 * j) % cohorts, f)
    for other in others:
        signal(c, other)
    pl.semaphore_wait(pltpu.get_barrier_semaphore(), cohorts // 2 + len(others))


def server_kernel(
    cohorts, gain, high, low, tokens, base, momentum, now, prev,
    all_ref, momentum_ref, fresh, got, to_far, to_pair, kept,
):
    lines = fresh.shape[1]

    def produce(piece):
        here = pl.ds(pl.multiple_of(piece * lines, lines), lines)
        both = lax.dot_general(
            jnp.concatenate([high[:, here], low[:, here]], axis=1),
            tokens[...],
            (((0,), (0,)), ((), ())),
            preferred_element_type=jnp.float32,
        )
        noise = (
            NOISE_STD
            * CLIP_BOUND
            * (now[here].astype(jnp.float32) - BAND_COEF * prev[here].astype(jnp.float32))
        )
        aggregate = gain * (both[:lines] + both[lines:] + noise)
        new_momentum = MOMENTUM_DECAY * momentum[here] + aggregate
        momentum_ref[here, :] = new_momentum
        fresh[pl.ds(piece, 1)] = (
            (base[here].astype(jnp.float32) + SERVER_LR * new_momentum).astype(fresh.dtype)[None]
        )

    greet(cohorts, lax.axis_index("cohort"), lax.axis_index("fsdp"), [])
    spread_kernel(cohorts, fresh, all_ref, got, to_far, to_pair, kept, produce=produce)


def serve(high, low, tokens, base, momentum, now, prev, gain, cohorts):
    hidden, width = base.shape
    lines = math.gcd(hidden, 128)
    pieces = hidden // lines
    return pl.pallas_call(
        lambda *refs: server_kernel(cohorts, gain, *refs),
        name="serve",
        out_shape=(
            jax.ShapeDtypeStruct((cohorts, pieces, lines, width), base.dtype),
            jax.ShapeDtypeStruct(momentum.shape, momentum.dtype),
        ),
        in_specs=[IN_VMEM] * 7,
        out_specs=(ANY, IN_VMEM),
        scratch_shapes=[
            pltpu.VMEM((pieces, lines, width), base.dtype),
            DMA((cohorts, pieces)),
            DMA((max(cohorts // 2 - 1, 1), pieces)),
            DMA((cohorts, pieces)),
            DMA,
        ],
        compiler_params=pltpu.CompilerParams(
            collective_id=2, has_side_effects=True, vmem_limit_bytes=60 << 20
        ),
    )(high, low, tokens, base, momentum, now, prev)


def errors_kernel(
    cohorts, shards, own_ref, part_ref, all_ref, norm_ref,
    got, to_far, to_pair, kept, parts, total, got_part, to_part, got_norm, to_norm,
):
    c, f = lax.axis_index("cohort"), lax.axis_index("fsdp")
    others = [(f + j) % shards for j in range(1, shards)]
    cohort_others = [(c + j) % cohorts for j in range(1, cohorts)]
    barrier = pltpu.get_barrier_semaphore()
    for other in others:
        signal(c, other)
    for other in cohort_others:
        signal(other, f)
    pl.semaphore_wait(barrier, len(others) + len(cohort_others))

    def part(at, source):
        return remote(part_ref, parts.at[source], to_part.at[at], got_part.at[source], c, others[at])

    def norm(at, source):
        return remote(
            total, norm_ref.at[source], to_norm.at[at], got_norm.at[source], cohort_others[at], f
        )

    def sum_norms():
        parts[pl.ds(f, 1)] = part_ref[...][None]
        for at, other in enumerate(others):
            part(at, other).wait_recv()
        summed = parts[0]
        for at in range(1, shards):
            summed = summed + parts[at]
        total[...] = summed
        norm_ref[pl.ds(c, 1)] = summed[None]
        for at in range(len(cohort_others)):
            norm(at, c).start()

    for at in range(len(others)):
        part(at, f).start()
    spread_kernel(cohorts, own_ref, all_ref, got, to_far, to_pair, kept, sum_norms)
    for at, other in enumerate(cohort_others):
        norm(at, other).wait_recv()
        norm(at, c).wait_send()
    for at in range(len(others)):
        part(at, f).wait_send()


def spread_errors(errors, squared, cohorts, shards):
    pieces = errors.shape[0]
    tile = jnp.broadcast_to(squared[:, None], (squared.shape[0], 128))
    return pl.pallas_call(
        lambda *refs: errors_kernel(cohorts, shards, *refs),
        name="spread_errors",
        out_shape=(
            jax.ShapeDtypeStruct((cohorts,) + errors.shape, errors.dtype),
            jax.ShapeDtypeStruct((cohorts,) + tile.shape, tile.dtype),
        ),
        in_specs=[IN_VMEM, IN_VMEM],
        out_specs=(ANY, IN_VMEM),
        scratch_shapes=[
            DMA((cohorts, pieces)),
            DMA((max(cohorts // 2 - 1, 1), pieces)),
            DMA((cohorts, pieces)),
            DMA,
            pltpu.VMEM((shards,) + tile.shape, tile.dtype),
            pltpu.VMEM(tile.shape, tile.dtype),
            DMA((shards,)),
            DMA((shards,)),
            DMA((cohorts,)),
            DMA((cohorts,)),
        ],
        compiler_params=pltpu.CompilerParams(
            collective_id=1, has_side_effects=True, vmem_limit_bytes=60 << 20
        ),
    )(errors, tile)


def client_errors(tokens, products, targets):
    clients, steps, count, depth = tokens.shape
    rate = LOCAL_LR / (count * math.sqrt(depth))
    scale = 1.0 / math.sqrt(depth)
    flat = tokens.reshape(clients, steps * count, depth)
    gram = jnp.einsum("ksd,ktd->kst", flat, flat, preferred_element_type=jnp.float32)
    errors = []
    for step in range(steps):
        preact = products[:, step]
        if step > 0:
            earlier = jnp.concatenate(errors, axis=1).astype(jnp.float32)
            cross = gram[:, step * count : (step + 1) * count, : step * count]
            preact = preact - rate * jnp.einsum(
                "kst,ktf->ksf", cross, earlier, precision=lax.Precision.HIGHEST
            )
        errors.append(errors_of(preact * scale, targets[:, step]))
    errors = jnp.concatenate(errors, axis=1)
    error_gram = jnp.einsum("ksf,ktf->kst", errors, errors, preferred_element_type=jnp.float32)
    squared = rate * rate * jnp.maximum(jnp.sum(error_gram * gram, axis=(1, 2)), 0.0)
    return errors, squared, rate


def split_scaled(errors, factors):
    scaled = errors.astype(jnp.float32) * factors
    high = scaled.astype(jnp.bfloat16)
    low = (scaled - high.astype(jnp.float32)).astype(jnp.bfloat16)
    hidden = errors.shape[-1]
    return high.reshape(-1, hidden), low.reshape(-1, hidden)


def weighted_sum(errors, factors, tokens):
    tokens = tokens.reshape(-1, tokens.shape[-1])
    dims = (((0,), (0,)), ((), ()))
    return sum(
        lax.dot_general(part, tokens, dims, preferred_element_type=jnp.float32)
        for part in split_scaled(errors, factors)
    )


def products_of(tokens, weights):
    return lax.dot_general(
        tokens, weights, (((1,), (1,)), ((), ())), preferred_element_type=jnp.float32
    )


def factor_body(client_tokens, targets, weights, momentum, noise_now, noise_prev):
    cohorts, shards = lax.axis_size("cohort"), lax.axis_size("fsdp")
    hidden, depth = weights.shape
    _, clients, steps, count, _ = client_tokens.shape
    pieces = max(clients * steps * count // 16, 1)
    gathered, columns = gather_tokens(
        client_tokens.reshape(pieces, -1, depth), cohorts, shards
    )
    products = products_of(gathered.reshape(-1, depth), weights)
    products = products.reshape(shards, clients, steps, count, hidden)
    products = products.transpose(1, 2, 0, 3, 4).reshape(clients, steps, shards * count, hidden)
    tokens = gathered.reshape(shards, clients, steps, count, depth)
    tokens = tokens.transpose(1, 2, 0, 3, 4).reshape(clients, steps, shards * count, depth)
    errors, squared, rate = client_errors(tokens, products, targets[0])
    errors = errors.reshape(clients, steps, shards, count, hidden).transpose(2, 0, 1, 3, 4)
    errors, squared = spread_errors(errors.reshape(shards, -1, hidden), squared, cohorts, shards)
    factors = -rate * clip_factor(squared[:, :, 0])
    errors = errors.reshape(cohorts, shards, clients, steps * count, hidden)
    high, low = split_scaled(errors, factors[:, None, :, None, None])
    owner_width = columns.shape[-1]
    owner_start = lax.axis_index("cohort") * owner_width
    base_part = lax.dynamic_slice_in_dim(weights, owner_start, owner_width, 1)
    gain = math.sqrt(hidden * shards * depth) / (cohorts * clients * CLIP_BOUND)
    blocks, new_momentum = serve(
        high,
        low,
        columns.reshape(-1, owner_width),
        base_part,
        momentum,
        noise_now,
        noise_prev,
        gain,
        cohorts,
    )
    blocks = blocks.reshape(cohorts, hidden, owner_width)
    new_weights = blocks.transpose(1, 0, 2).reshape(hidden, depth)
    return (new_weights, new_momentum)


def sum_body(client_tokens, targets, weights, momentum, noise_now, noise_prev):
    depth = weights.shape[1]
    clients = client_tokens.shape[1]
    round_block = lax.all_gather(client_tokens[0], "fsdp", axis=2, tiled=True)
    products = products_of(round_block.reshape(-1, depth), weights)
    products = products.reshape(round_block.shape[:3] + weights.shape[:1])
    errors, squared, rate = client_errors(round_block, products, targets[0])
    squared = lax.psum(squared, "fsdp")
    cohort_sum = weighted_sum(
        errors, (-rate * clip_factor(squared))[:, None, None], round_block
    )
    totals = lax.psum_scatter(cohort_sum, "cohort", scatter_dimension=1, tiled=True)
    owner_width = totals.shape[1]
    owner_start = lax.axis_index("cohort") * owner_width
    base_part = lax.dynamic_slice_in_dim(weights, owner_start, owner_width, 1).astype(jnp.float32)
    cohort_count = lax.axis_size("cohort")
    hidden_count = weights.shape[0] * lax.axis_size("fsdp")
    noise = (
        NOISE_STD
        * CLIP_BOUND
        * (noise_now.astype(jnp.float32) - BAND_COEF * noise_prev.astype(jnp.float32))
    )
    aggregate = (
        math.sqrt(hidden_count * depth) / (cohort_count * clients * CLIP_BOUND) * (totals + noise)
    )
    new_momentum = MOMENTUM_DECAY * momentum + aggregate
    new_part = (base_part + SERVER_LR * new_momentum).astype(jnp.bfloat16)
    new_weights = lax.all_gather(new_part, "cohort", axis=1, tiled=True)
    return (new_weights, new_momentum)


def body(client_tokens, *others):
    _, clients, steps, count, _ = client_tokens.shape
    hidden = others[1].shape[0]
    rank = clients * steps * count * lax.axis_size("fsdp")
    few = rank <= hidden and lax.axis_size("cohort") % 2 == 0 and lax.axis_size("fsdp") % 2 == 0
    return (factor_body if few else sum_body)(client_tokens, *others)


def solution(mesh):
    in_specs = (
        P("cohort", None, None, "fsdp", None),
        P("cohort", None, None, None, "fsdp"),
        P("fsdp", None),
        P("fsdp", "cohort"),
        P("fsdp", "cohort"),
        P("fsdp", "cohort"),
    )
    out_specs = (P("fsdp", None), P("fsdp", "cohort"))
    return jax.shard_map(body, mesh=mesh, in_specs=in_specs, out_specs=out_specs, check_vma=False)
```

```python
import math

import jax
import jax.numpy as jnp
from jax import lax
from jax.experimental import pallas as pl
from jax.experimental.pallas import tpu as pltpu
from jax.sharding import PartitionSpec as P

LOCAL_LR = 300.0
CLIP_BOUND = 32.0
NOISE_STD = 0.0004
BAND_COEF = 0.5
MOMENTUM_DECAY = 0.9
SERVER_LR = 0.5
EPSILON = 1e-06


def gelu_parts(preact):
    inner = 0.7978845608 * (preact + 0.044715 * preact * preact * preact)
    tangent = jnp.tanh(inner)
    activation = 0.5 * preact * (1.0 + tangent)
    slope = 0.5 * (1.0 + tangent) + 0.5 * preact * (1.0 - tangent * tangent) * 0.7978845608 * (
        1.0 + 3.0 * 0.044715 * preact * preact
    )
    return (activation, slope)


def clip_factor(squared):
    return jnp.minimum(1.0, CLIP_BOUND / (jnp.sqrt(squared) + EPSILON))


def errors_of(preact, targets):
    activation, slope = gelu_parts(preact)
    return ((activation - targets.astype(jnp.float32)) * slope).astype(jnp.bfloat16)


MESH = pl.DeviceIdType.MESH
ANY = pl.BlockSpec(memory_space=pl.ANY)
IN_VMEM = pl.BlockSpec(memory_space=pltpu.VMEM)
DMA = pltpu.SemaphoreType.DMA


def remote(source, target, send, receive, cohort, fsdp):
    return pltpu.make_async_remote_copy(
        src_ref=source,
        dst_ref=target,
        send_sem=send,
        recv_sem=receive,
        device_id={"cohort": cohort, "fsdp": fsdp},
        device_id_type=MESH,
    )


def signal(cohort, fsdp):
    pl.semaphore_signal(
        pltpu.get_barrier_semaphore(),
        inc=1,
        device_id={"cohort": cohort, "fsdp": fsdp},
        device_id_type=MESH,
    )


def gather_kernel(
    cohorts, shards, own_ref, all_ref, cut_ref, got, got_cut, to_up, to_down, to_pair, to_cut, kept, kept_cut
):
    c, f = lax.axis_index("cohort"), lax.axis_index("fsdp")
    rows = shards // 2
    row, side = f // 2, f % 2
    pair = f + 1 - 2 * side
    width = cut_ref.shape[-1]
    others = [(c + j) % cohorts for j in range(1, cohorts)]

    signal(c, (f + 2) % shards)
    signal(c, (f + shards - 2) % shards)
    signal(c, pair)
    for other in others:
        signal(other, f)
    pl.semaphore_wait(pltpu.get_barrier_semaphore(), cohorts + 2)

    pieces = own_ref.shape[0]

    def up(slot, piece, source):
        return remote(
            source, all_ref.at[slot, piece], to_up.at[slot, piece], got.at[slot, piece], c, f + 2
        )

    def down(slot, piece, source):
        return remote(
            source, all_ref.at[slot, piece], to_down.at[slot, piece], got.at[slot, piece], c, f - 2
        )

    def across(slot, piece, source):
        return remote(
            source, all_ref.at[slot, piece], to_pair.at[slot, piece], got.at[slot, piece], c, pair
        )

    def columns(source, owner):
        return source.at[:, pl.ds(pl.multiple_of(owner * width, 128), width)]

    def cuts(slot, piece, source):
        copies = [
            remote(
                columns(source, other),
                cut_ref.at[c, slot, piece],
                to_cut.at[at, slot, piece],
                got_cut.at[c, slot, piece],
                other,
                f,
            )
            for at, other in enumerate(others)
        ]
        own = pltpu.make_async_copy(
            columns(source, c), cut_ref.at[c, slot, piece], kept_cut.at[slot, piece]
        )
        return copies + [own]

    def arrived(slot, piece):
        across(slot, piece, own_ref.at[0]).wait_recv()

    def start(copies):
        for copy in copies:
            copy.start()

    keep = pltpu.make_async_copy(own_ref, all_ref.at[f], kept)
    for piece in range(pieces):

        @pl.when(row + 1 < rows)
        def _():
            up(f, piece, own_ref.at[piece]).start()

        @pl.when(row > 0)
        def _():
            down(f, piece, own_ref.at[piece]).start()

        across(f, piece, own_ref.at[piece]).start()
        start(cuts(f, piece, own_ref.at[piece]))
    keep.start()

    for step in range(1, rows + 1):
        last = step - 1
        for piece in range(pieces):

            @pl.when(row >= step)
            def _():
                slot = f - 2 * step
                arrived(slot, piece)

                @pl.when(row + 1 < rows)
                def _():
                    up(slot, piece, all_ref.at[slot, piece]).start()

                across(slot, piece, all_ref.at[slot, piece]).start()
                start(cuts(slot, piece, all_ref.at[slot, piece]))

            @pl.when(row + step < rows)
            def _():
                slot = f + 2 * step
                arrived(slot, piece)

                @pl.when(row > 0)
                def _():
                    down(slot, piece, all_ref.at[slot, piece]).start()

                across(slot, piece, all_ref.at[slot, piece]).start()
                start(cuts(slot, piece, all_ref.at[slot, piece]))

            @pl.when(row >= last)
            def _():
                slot = pair - 2 * last
                arrived(slot, piece)
                start(cuts(slot, piece, all_ref.at[slot, piece]))

            if last > 0:

                @pl.when(row + last < rows)
                def _():
                    slot = pair + 2 * last
                    arrived(slot, piece)
                    start(cuts(slot, piece, all_ref.at[slot, piece]))

    keep.wait()
    for piece in range(pieces):
        source = own_ref.at[piece]
        for line in range(rows):
            slot = 2 * line + side

            @pl.when((row + 1 < rows) & (line <= row))
            def _():
                up(slot, piece, source).wait_send()

            @pl.when((row > 0) & (line >= row))
            def _():
                down(slot, piece, source).wait_send()

            across(slot, piece, source).wait_send()
        for slot in range(shards):
            *sent, own = cuts(slot, piece, source)
            own.wait()
            for copy in sent:
                copy.wait_send()
            for other in others:
                remote(
                    columns(source, c),
                    cut_ref.at[other, slot, piece],
                    to_pair.at[slot, piece],
                    got_cut.at[other, slot, piece],
                    other,
                    f,
                ).wait_recv()


def gather_tokens(tokens, cohorts, shards):
    pieces, count, depth = tokens.shape
    return pl.pallas_call(
        lambda *refs: gather_kernel(cohorts, shards, *refs),
        name="gather_tokens",
        out_shape=(
            jax.ShapeDtypeStruct((shards, pieces, count, depth), tokens.dtype),
            jax.ShapeDtypeStruct((cohorts, shards, pieces, count, depth // cohorts), tokens.dtype),
        ),
        in_specs=[IN_VMEM],
        out_specs=(IN_VMEM, ANY),
        scratch_shapes=[
            DMA((shards, pieces)),
            DMA((cohorts, shards, pieces)),
            DMA((shards, pieces)),
            DMA((shards, pieces)),
            DMA((shards, pieces)),
            DMA((cohorts - 1, shards, pieces)),
            DMA,
            DMA((shards, pieces)),
        ],
        compiler_params=pltpu.CompilerParams(
            collective_id=0, has_side_effects=True, vmem_limit_bytes=60 << 20
        ),
    )(tokens)


def spread_kernel(cohorts, own_ref, all_ref, got, to_far, to_pair, kept, meanwhile=None, produce=None):
    c, f = lax.axis_index("cohort"), lax.axis_index("fsdp")
    pair = c + 1 - 2 * (c % 2)
    pieces = own_ref.shape[0]
    far = [(c + 2 * j) % cohorts for j in range(1, cohorts // 2)]
    keep = pltpu.make_async_copy(own_ref, all_ref.at[c], kept)
    if produce is None:
        keep.start()

    def outward(at, piece):
        return remote(
            own_ref.at[piece],
            all_ref.at[c, piece],
            to_far.at[at, piece],
            got.at[c, piece],
            far[at],
            f,
        )

    def across(slot, piece, source):
        return remote(
            source, all_ref.at[slot, piece], to_pair.at[slot, piece], got.at[slot, piece], pair, f
        )

    def send(piece):
        if produce is not None:
            produce(piece)
        for at in range(len(far)):
            outward(at, piece).start()
        across(c, piece, own_ref.at[piece]).start()

    if produce is None:
        for piece in range(pieces):
            send(piece)
    else:
        pl.loop(0, pieces)(send)
        keep.start()
    if meanwhile is not None:
        meanwhile()
    for piece in range(pieces):
        for slot in far:
            copy = across(slot, piece, all_ref.at[slot, piece])
            copy.wait_recv()
            copy.start()
    for piece in range(pieces):
        for at in range(len(far)):
            outward(at, piece).wait_send()
        for slot in [c] + far:
            across(slot, piece, own_ref.at[piece]).wait_send()
        for j in range(cohorts // 2):
            slot = (pair + 2 * j) % cohorts
            across(slot, piece, own_ref.at[piece]).wait_recv()
    keep.wait()


def greet(cohorts, c, f, others):
    signal(c + 1 - 2 * (c % 2), f)
    for j in range(1, cohorts // 2):
        signal((c + 2 * j) % cohorts, f)
    for other in others:
        signal(c, other)
    pl.semaphore_wait(pltpu.get_barrier_semaphore(), cohorts // 2 + len(others))


def server_kernel(
    cohorts, gain, errors, factors, tokens, weights, momentum, now, prev,
    all_ref, momentum_ref, fresh, base, fetched, got, to_far, to_pair, kept,
):
    lines = fresh.shape[1]

    def produce(piece):
        here = pl.ds(pl.multiple_of(piece * lines, lines), lines)
        scaled = errors[:, here].astype(jnp.float32) * factors[...]
        high = scaled.astype(jnp.bfloat16)
        low = (scaled - high.astype(jnp.float32)).astype(jnp.bfloat16)
        both = lax.dot_general(
            jnp.concatenate([high, low], axis=1),
            tokens[...],
            (((0,), (0,)), ((), ())),
            preferred_element_type=jnp.float32,
        )
        noise = (
            NOISE_STD
            * CLIP_BOUND
            * (now[here].astype(jnp.float32) - BAND_COEF * prev[here].astype(jnp.float32))
        )
        aggregate = gain * (both[:lines] + both[lines:] + noise)
        new_momentum = MOMENTUM_DECAY * momentum[here] + aggregate
        momentum_ref[here, :] = new_momentum
        fresh[pl.ds(piece, 1)] = (
            (base[here].astype(jnp.float32) + SERVER_LR * new_momentum).astype(fresh.dtype)[None]
        )

    width = base.shape[1]
    start = pl.multiple_of(lax.axis_index("cohort") * width, 128)
    fetch = pltpu.make_async_copy(weights.at[:, pl.ds(start, width)], base, fetched)
    fetch.start()
    greet(cohorts, lax.axis_index("cohort"), lax.axis_index("fsdp"), [])
    fetch.wait()
    spread_kernel(cohorts, fresh, all_ref, got, to_far, to_pair, kept, produce=produce)


def serve(errors, factors, tokens, weights, momentum, now, prev, gain, cohorts):
    hidden, width = momentum.shape
    lines = math.gcd(hidden, 128)
    pieces = hidden // lines
    factors = jnp.broadcast_to(factors, errors.shape[:-1] + (lines,)).reshape(-1, lines)
    return pl.pallas_call(
        lambda *refs: server_kernel(cohorts, gain, *refs),
        name="serve",
        out_shape=(
            jax.ShapeDtypeStruct((cohorts, pieces, lines, width), weights.dtype),
            jax.ShapeDtypeStruct(momentum.shape, momentum.dtype),
        ),
        in_specs=[IN_VMEM] * 3 + [ANY] + [IN_VMEM] * 3,
        out_specs=(ANY, IN_VMEM),
        scratch_shapes=[
            pltpu.VMEM((pieces, lines, width), weights.dtype),
            pltpu.VMEM((hidden, width), weights.dtype),
            DMA,
            DMA((cohorts, pieces)),
            DMA((max(cohorts // 2 - 1, 1), pieces)),
            DMA((cohorts, pieces)),
            DMA,
        ],
        compiler_params=pltpu.CompilerParams(
            collective_id=2, has_side_effects=True, vmem_limit_bytes=60 << 20
        ),
    )(errors.reshape(-1, hidden), factors, tokens, weights, momentum, now, prev)


def errors_kernel(
    cohorts, shards, own_ref, part_ref, all_ref, norm_ref,
    got, to_far, to_pair, kept, parts, total, got_part, to_part, got_norm, to_norm,
):
    c, f = lax.axis_index("cohort"), lax.axis_index("fsdp")
    others = [(f + j) % shards for j in range(1, shards)]
    cohort_others = [(c + j) % cohorts for j in range(1, cohorts)]
    barrier = pltpu.get_barrier_semaphore()
    for other in others:
        signal(c, other)
    for other in cohort_others:
        signal(other, f)
    pl.semaphore_wait(barrier, len(others) + len(cohort_others))

    def part(at, source):
        return remote(part_ref, parts.at[source], to_part.at[at], got_part.at[source], c, others[at])

    def norm(at, source):
        return remote(
            total, norm_ref.at[source], to_norm.at[at], got_norm.at[source], cohort_others[at], f
        )

    def sum_norms():
        parts[pl.ds(f, 1)] = part_ref[...][None]
        for at, other in enumerate(others):
            part(at, other).wait_recv()
        summed = parts[0]
        for at in range(1, shards):
            summed = summed + parts[at]
        total[...] = summed
        norm_ref[pl.ds(c, 1)] = summed[None]
        for at in range(len(cohort_others)):
            norm(at, c).start()

    for at in range(len(others)):
        part(at, f).start()
    spread_kernel(cohorts, own_ref, all_ref, got, to_far, to_pair, kept, sum_norms)
    for at, other in enumerate(cohort_others):
        norm(at, other).wait_recv()
        norm(at, c).wait_send()
    for at in range(len(others)):
        part(at, f).wait_send()


def spread_errors(errors, squared, cohorts, shards):
    pieces = errors.shape[0]
    tile = jnp.broadcast_to(squared[:, None], (squared.shape[0], 128))
    return pl.pallas_call(
        lambda *refs: errors_kernel(cohorts, shards, *refs),
        name="spread_errors",
        out_shape=(
            jax.ShapeDtypeStruct((cohorts,) + errors.shape, errors.dtype),
            jax.ShapeDtypeStruct((cohorts,) + tile.shape, tile.dtype),
        ),
        in_specs=[IN_VMEM, IN_VMEM],
        out_specs=(ANY, IN_VMEM),
        scratch_shapes=[
            DMA((cohorts, pieces)),
            DMA((max(cohorts // 2 - 1, 1), pieces)),
            DMA((cohorts, pieces)),
            DMA,
            pltpu.VMEM((shards,) + tile.shape, tile.dtype),
            pltpu.VMEM(tile.shape, tile.dtype),
            DMA((shards,)),
            DMA((shards,)),
            DMA((cohorts,)),
            DMA((cohorts,)),
        ],
        compiler_params=pltpu.CompilerParams(
            collective_id=1, has_side_effects=True, vmem_limit_bytes=60 << 20
        ),
    )(errors, tile)


def client_errors(tokens, products, targets):
    clients, steps, count, depth = tokens.shape
    rate = LOCAL_LR / (count * math.sqrt(depth))
    scale = 1.0 / math.sqrt(depth)
    flat = tokens.reshape(clients, steps * count, depth)
    gram = jnp.einsum("ksd,ktd->kst", flat, flat, preferred_element_type=jnp.float32)
    errors = []
    for step in range(steps):
        preact = products[:, step]
        if step > 0:
            earlier = jnp.concatenate(errors, axis=1).astype(jnp.float32)
            cross = gram[:, step * count : (step + 1) * count, : step * count]
            preact = preact - rate * jnp.einsum(
                "kst,ktf->ksf", cross, earlier, precision=lax.Precision.HIGHEST
            )
        errors.append(errors_of(preact * scale, targets[:, step]))
    errors = jnp.concatenate(errors, axis=1)
    error_gram = jnp.einsum("ksf,ktf->kst", errors, errors, preferred_element_type=jnp.float32)
    squared = rate * rate * jnp.maximum(jnp.sum(error_gram * gram, axis=(1, 2)), 0.0)
    return errors, squared, rate


def split_scaled(errors, factors):
    scaled = errors.astype(jnp.float32) * factors
    high = scaled.astype(jnp.bfloat16)
    low = (scaled - high.astype(jnp.float32)).astype(jnp.bfloat16)
    hidden = errors.shape[-1]
    return high.reshape(-1, hidden), low.reshape(-1, hidden)


def weighted_sum(errors, factors, tokens):
    tokens = tokens.reshape(-1, tokens.shape[-1])
    dims = (((0,), (0,)), ((), ()))
    return sum(
        lax.dot_general(part, tokens, dims, preferred_element_type=jnp.float32)
        for part in split_scaled(errors, factors)
    )


def products_of(tokens, weights):
    return lax.dot_general(
        tokens, weights, (((1,), (1,)), ((), ())), preferred_element_type=jnp.float32
    )


def factor_body(client_tokens, targets, weights, momentum, noise_now, noise_prev):
    cohorts, shards = lax.axis_size("cohort"), lax.axis_size("fsdp")
    hidden, depth = weights.shape
    _, clients, steps, count, _ = client_tokens.shape
    pieces = max(clients * steps * count // 16, 1)
    gathered, columns = gather_tokens(
        client_tokens.reshape(pieces, -1, depth), cohorts, shards
    )
    products = products_of(gathered.reshape(-1, depth), weights)
    products = products.reshape(shards, clients, steps, count, hidden)
    products = products.transpose(1, 2, 0, 3, 4).reshape(clients, steps, shards * count, hidden)
    tokens = gathered.reshape(shards, clients, steps, count, depth)
    tokens = tokens.transpose(1, 2, 0, 3, 4).reshape(clients, steps, shards * count, depth)
    errors, squared, rate = client_errors(tokens, products, targets[0])
    errors = errors.reshape(clients, steps, shards, count, hidden).transpose(2, 0, 1, 3, 4)
    errors, squared = spread_errors(errors.reshape(shards, -1, hidden), squared, cohorts, shards)
    factors = -rate * clip_factor(squared[:, :, 0])
    errors = errors.reshape(cohorts, shards, clients, steps * count, hidden)
    owner_width = columns.shape[-1]
    gain = math.sqrt(hidden * shards * depth) / (cohorts * clients * CLIP_BOUND)
    blocks, new_momentum = serve(
        errors,
        factors[:, None, :, None, None],
        columns.reshape(-1, owner_width),
        weights,
        momentum,
        noise_now,
        noise_prev,
        gain,
        cohorts,
    )
    blocks = blocks.reshape(cohorts, hidden, owner_width)
    new_weights = blocks.transpose(1, 0, 2).reshape(hidden, depth)
    return (new_weights, new_momentum)


def sum_body(client_tokens, targets, weights, momentum, noise_now, noise_prev):
    depth = weights.shape[1]
    clients = client_tokens.shape[1]
    round_block = lax.all_gather(client_tokens[0], "fsdp", axis=2, tiled=True)
    products = products_of(round_block.reshape(-1, depth), weights)
    products = products.reshape(round_block.shape[:3] + weights.shape[:1])
    errors, squared, rate = client_errors(round_block, products, targets[0])
    squared = lax.psum(squared, "fsdp")
    cohort_sum = weighted_sum(
        errors, (-rate * clip_factor(squared))[:, None, None], round_block
    )
    totals = lax.psum_scatter(cohort_sum, "cohort", scatter_dimension=1, tiled=True)
    owner_width = totals.shape[1]
    owner_start = lax.axis_index("cohort") * owner_width
    base_part = lax.dynamic_slice_in_dim(weights, owner_start, owner_width, 1).astype(jnp.float32)
    cohort_count = lax.axis_size("cohort")
    hidden_count = weights.shape[0] * lax.axis_size("fsdp")
    noise = (
        NOISE_STD
        * CLIP_BOUND
        * (noise_now.astype(jnp.float32) - BAND_COEF * noise_prev.astype(jnp.float32))
    )
    aggregate = (
        math.sqrt(hidden_count * depth) / (cohort_count * clients * CLIP_BOUND) * (totals + noise)
    )
    new_momentum = MOMENTUM_DECAY * momentum + aggregate
    new_part = (base_part + SERVER_LR * new_momentum).astype(jnp.bfloat16)
    new_weights = lax.all_gather(new_part, "cohort", axis=1, tiled=True)
    return (new_weights, new_momentum)


def body(client_tokens, *others):
    _, clients, steps, count, _ = client_tokens.shape
    hidden = others[1].shape[0]
    rank = clients * steps * count * lax.axis_size("fsdp")
    few = rank <= hidden and lax.axis_size("cohort") % 2 == 0 and lax.axis_size("fsdp") % 2 == 0
    return (factor_body if few else sum_body)(client_tokens, *others)


def solution(mesh):
    in_specs = (
        P("cohort", None, None, "fsdp", None),
        P("cohort", None, None, None, "fsdp"),
        P("fsdp", None),
        P("fsdp", "cohort"),
        P("fsdp", "cohort"),
        P("fsdp", "cohort"),
    )
    out_specs = (P("fsdp", None), P("fsdp", "cohort"))
    return jax.shard_map(body, mesh=mesh, in_specs=in_specs, out_specs=out_specs, check_vma=False)
```
